32 devices in a mesh: sector: 8 (over z, x), mpo: 4 (over y, core).
Axes of the slice: x: 2, y: 2, z: 4, core: 2. Of those that a mesh axis runs over, the one named last changes fastest.
Arguments:
- psi: float32 [8, 768, 768], P('sector'), may hold values from -24 to 24, as said below
- left_env: float32 [4, 8, 768, 768], P('mpo', 'sector'), may hold values from -0.21875 to 0.21875
- right_env: float32 [4, 8, 768, 768], P('mpo', 'sector'), may hold values from -0.21875 to 0.21875
- sector_label: int32 [8], replicated, may hold values from 0 to 7, as said below
- charge_step: int32 [4, 8, 3], replicated, may hold values from -1 to 1
- coef_index: int32 [4, 8, 3], replicated, may hold values from 0 to 7
- entry_values: float32 [8], replicated, may hold values from -1.5 to 1.5
- recurrence: float32 [3], replicated, may hold values from -2 to 2
Outputs:
- vec_one: float32 [8, 768, 768], P('sector')
- vec_two: float32 [8, 768, 768], P('sector')
The draws below stay inside these ranges and needn't reach their ends.
Inputs may be any that keep to these rules, and one draw needn't show every extreme that they name: `psi`: each sector block's entries lie in this range. `sector_label`: A permutation of the labels over the slots; two sectors whose labels differ by one lie at most 3 slots apart.
All inputs are finite; a program needn't handle non-finite values.
Results may differ from the reference program's by a relative error of at most 0.0029.
Values may be sent and summed in bfloat16 or wider, within the bound.
A program may use at most 64 MiB of HBM per device.

```python
import jax
import jax.numpy as jnp
from jax import lax

M = 768
K = 3
NCOEF = 8
SECTORS = 8
MPO_BOND = 4


def draw_psi(key, part):
    key_base, key_jitter = jax.random.split(key, 2)
    ramp_up = jnp.exp(jnp.log(3.0) * jnp.arange(SECTORS, dtype=jnp.float32) / (SECTORS - 1))
    jitter = jax.random.uniform(key_jitter, (SECTORS,), jnp.float32, 0.7, 1.3)
    base = jnp.clip(jax.random.normal(key_base, (SECTORS, M, M), jnp.float32), -6.0, 6.0)
    scales = ramp_up * jitter
    return base * scales[:, None, None]


def draw_sector_label(key, part):
    pair_count = SECTORS // 2
    swap_bits = jax.random.randint(jax.random.fold_in(key, 7), (pair_count,), 0, 2)
    forced = jax.random.randint(jax.random.fold_in(key, 11), (), 0, pair_count - 1)
    pair_ids = jnp.arange(pair_count, dtype=jnp.int32)
    swap_bits = jnp.where((pair_ids == forced) | (pair_ids == forced + 1), 1, swap_bits)
    mirror = jax.random.randint(jax.random.fold_in(key, 13), (), 0, 2)
    slots = jnp.arange(SECTORS, dtype=jnp.int32)
    per_slot = jnp.repeat(swap_bits, 2)
    labels = slots + per_slot * (1 - 2 * (slots % 2))
    labels = jnp.where(mirror == 1, SECTORS - 1 - labels, labels)
    return labels.astype(jnp.int32)


def plant(result, rng, smallest, largest):
    spot = [jax.random.randint(jax.random.fold_in(rng, axis), (), 0, length) for axis, length in enumerate(result.shape)]
    widest = result.shape.index(max(result.shape))
    neighbour = spot[:widest] + [(spot[widest] + 1) % result.shape[widest]] + spot[widest + 1:]
    return result.at[tuple(spot)].set(smallest).at[tuple(neighbour)].set(largest)


def block_scale(stream_key, dims, pieces, least, top_value):
    level, own = 1.0, jax.random.fold_in(stream_key, 6)
    for axis_at, parts in pieces:
        steps = jnp.exp(jax.random.uniform(jax.random.fold_in(own, axis_at), (parts,), jnp.float32, least / len(pieces), top_value / len(pieces)))
        level = level * jnp.repeat(steps, dims[axis_at] // parts).reshape([-1 if axis == axis_at else 1 for axis in range(len(dims))])
    return level


def scatter_about(rng, shape, scale, bound, cuts=(), kind=jnp.bfloat16):
    array = scale * jax.random.normal(rng, shape, jnp.float32)
    if cuts:
        array = array * block_scale(rng, shape, cuts, -0.22, 0.18)
    return jnp.clip(array, -bound, bound).astype(kind)


def setup_inputs(seed: int = 0) -> dict:
    splits = jax.random.split(jax.random.key(seed), 9)
    psi = draw_psi(jax.random.fold_in(splits[8], 71), 0)
    left_env = scatter_about(splits[1], (MPO_BOND, SECTORS, M, M), M ** -0.5, 0.21875, ((0, 4), (1, 8)), jnp.float32)
    right_env = scatter_about(splits[2], (MPO_BOND, SECTORS, M, M), M ** -0.5, 0.21875, ((0, 4), (1, 8)), jnp.float32)
    sector_label = draw_sector_label(jax.random.fold_in(splits[8], 71), 0)
    charge_step = plant(jax.random.randint(splits[4], (MPO_BOND, SECTORS, K), -1, 2), jax.random.fold_in(splits[4], 1), -1, 1).astype(jnp.int32)
    coef_index = plant(jax.random.randint(splits[5], (MPO_BOND, SECTORS, K), 0, NCOEF), jax.random.fold_in(splits[5], 1), 0, NCOEF - 1).astype(jnp.int32)
    entry_values = jnp.clip(jax.random.uniform(splits[6], (NCOEF,), jnp.float32, -1.5, 1.5), -1.5, 1.5)
    recurrence = jnp.clip(jax.random.uniform(splits[7], (3,), jnp.float32, -2.0, 2.0), -2.0, 2.0)
    return {"psi": psi, "left_env": left_env, "right_env": right_env, "sector_label": sector_label, "charge_step": charge_step, "coef_index": coef_index, "entry_values": entry_values, "recurrence": recurrence}


EPS = 1e-06
highest = lax.Precision.HIGHEST

def coupling_table(sector_label, charge_step, coef_index, entry_values):
    target = sector_label[None, :, None] + charge_step
    table = jnp.arange(entry_values.shape[0], dtype=jnp.int32)
    values = lax.optimization_barrier(jnp.sum(jnp.where(coef_index[..., None] == table, entry_values, jnp.float32(0.0)), axis=-1))
    matches = target[..., None] == sector_label[None, None, None, :]
    return lax.optimization_barrier(jnp.sum(jnp.where(matches, values[..., None], jnp.float32(0.0)), axis=2))

def apply_hamiltonian(vector, left_env, right_env, couple):

    def step_bond(summed, inputs):
        left_bond, right_bond, couple_bond = inputs
        product = jnp.einsum('sab,sbc->sac', left_bond, vector, precision=highest).astype(jnp.bfloat16)
        mixed = jnp.einsum('ji,jab->iab', couple_bond, product.astype(jnp.float32), precision=highest)
        return (summed + jnp.einsum('iab,ibc->iac', mixed, right_bond, precision=highest), None)
    summed, unused = lax.scan(step_bond, jnp.zeros(vector.shape, jnp.float32), (left_env, right_env, couple))
    return summed

def normalize(resid):
    return resid / jnp.sqrt(jnp.mean(resid * resid) + EPS)

def reference(psi, left_env, right_env, sector_label, charge_step, coef_index, entry_values, recurrence):
    couple = coupling_table(sector_label, charge_step, coef_index, entry_values)
    first = apply_hamiltonian(psi, left_env, right_env, couple)
    vec_one = normalize(first - recurrence[0] * psi)
    second = apply_hamiltonian(vec_one, left_env, right_env, couple)
    vec_two = normalize(second - recurrence[1] * vec_one - recurrence[2] * psi)
    return (vec_one, vec_two)
```

```python
import functools

import jax
import jax.numpy as jnp
from jax import lax
from jax.experimental import pallas as pl
from jax.experimental.pallas import tpu as pltpu
from jax.sharding import PartitionSpec as P

EPS = 1e-06
LINK_CHUNKS, FULL_CHUNKS, LOADS = 12, 3, 6
FROM_PARTNER, FROM_BELOW, FROM_ABOVE, PARTNER_RELAY, ABOVE_RELAY, BELOW_RELAY = range(6)
MESH = pl.DeviceIdType.MESH
f32, bf16 = jnp.float32, jnp.bfloat16


def split(value):
    high = value.astype(bf16)
    return high, (value - high.astype(f32)).astype(bf16)


def dot_split(left, right_high, right_low):
    high, low = split(left)
    dot = functools.partial(jnp.dot, preferred_element_type=f32)
    return dot(high, right_high) + (dot(low, right_high) + dot(high, right_low))


def kernel(
    lean, chunks, sectors, bonds, cells,
    label_ref, step_ref, index_ref, entry_ref, coef_ref, left_ref, right_ref, psi_ref,
    one_ref, two_ref,
    hi, lo, right_hi, right_lo, own, pick, slots, term, half_in, half, part_in, resid, squares, parts, sums,
    x_send, x_recv, p_send, p_recv, y_send, y_recv, g_send, g_recv, h_send, h_recv, q_send, q_recv, s_send, s_recv,
):
    sector, bond = lax.axis_index("sector"), lax.axis_index("mpo")
    width = left_ref.shape[0]
    rows = width // chunks
    pair_rows = rows // 2
    stacks = bonds // 2
    part_rows = pair_rows // stacks
    core, stack = lax.rem(bond, 2), bond // 2
    sign = 1 - 2 * lax.rem(sector, 2)
    partner, ahead, behind = sector + sign, sector + 2 * sign, sector - 2 * sign
    has_ahead = (ahead >= 0) & (ahead < sectors)
    has_behind = (behind >= 0) & (behind < sectors)
    has_far = (sector - 4 * sign >= 0) & (sector - 4 * sign < sectors)
    other_core = stack * 2 + 1 - core
    entries = step_ref.shape[0]

    def stack_at(step):
        return lax.rem(stack + step, stacks) * 2 + core

    barrier = pltpu.get_barrier_semaphore()
    for step in range(1, sectors):
        pl.semaphore_signal(
            barrier, inc=1, device_id=(lax.rem(sector + step, sectors), bond), device_id_type=MESH
        )
    for step in range(1, bonds):
        pl.semaphore_signal(
            barrier, inc=1, device_id=(sector, lax.rem(bond + step, bonds)), device_id_type=MESH
        )

    def inside(slot):
        return jnp.minimum(jnp.maximum(slot, 0), sectors - 1)

    own_label = label_ref[sector]

    def couple(source):
        slot = inside(source)
        label = label_ref[slot]
        total = f32(0.0)
        for entry in range(entries):
            match = label + step_ref[entry, bond, slot] == own_label
            value = entry_ref[index_ref[entry, bond, slot]]
            total = total + jnp.where(match, value, f32(0.0))
        return jnp.where(source == slot, total, f32(0.0))

    def adjacent(slot):
        gap = label_ref[inside(slot)] - own_label
        return (gap == 1) | (gap == -1)

    own_weight = couple(sector)
    if lean:
        takes = (jnp.where(adjacent(ahead), f32(1.0), f32(0.0)),
                 jnp.where(adjacent(behind), f32(1.0), f32(0.0)))
        weights = (
            couple(partner),
            jnp.where(adjacent(behind), couple(behind), couple(behind + sign)),
            jnp.where(adjacent(ahead), couple(ahead), couple(ahead + sign)),
        )
    else:
        weights = tuple(couple(sector + sign * place) for place in (1, -2, 2, -1, 3, -3))

    def send(source, target, send_sem, recv_sem, device):
        return pltpu.make_async_remote_copy(
            src_ref=source, dst_ref=target, send_sem=send_sem, recv_sem=recv_sem,
            device_id=device, device_id_type=MESH,
        )

    def block_copy(kind, c):
        here = pl.ds(pl.multiple_of(c * rows, rows), rows)
        source, device = {
            FROM_PARTNER: (own, partner),
            FROM_BELOW: (pick.at[0] if lean else own, ahead),
            FROM_ABOVE: (pick.at[1] if lean else own, behind),
            PARTNER_RELAY: (slots.at[FROM_ABOVE], partner),
            ABOVE_RELAY: (slots.at[FROM_PARTNER], behind),
            BELOW_RELAY: (slots.at[min(PARTNER_RELAY, len(weights) - 1)], ahead),
        }[kind]
        return send(
            source.at[here], slots.at[kind, here], x_send.at[kind, c], x_recv.at[kind, c],
            (device, bond),
        )

    sends_if = {
        FROM_PARTNER: None, FROM_BELOW: has_ahead, FROM_ABOVE: has_behind,
        PARTNER_RELAY: has_ahead, ABOVE_RELAY: has_behind, BELOW_RELAY: has_ahead & has_behind,
    }
    gets_if = {
        FROM_PARTNER: None, FROM_BELOW: has_behind, FROM_ABOVE: has_ahead,
        PARTNER_RELAY: has_behind, ABOVE_RELAY: has_ahead, BELOW_RELAY: has_far,
    }

    def when(condition, action):
        if condition is None:
            action()
        else:
            pl.when(condition)(action)

    def start(kind, c):
        when(sends_if[kind], lambda: block_copy(kind, c).start())

    def arrive(kind, c):
        when(gets_if[kind], lambda: block_copy(kind, c).wait_recv())

    def pair_copy(c):
        there = c * rows + (1 - core) * pair_rows
        there = pl.ds(pl.multiple_of(there, 8), pair_rows)
        return send(
            term.at[there], half_in.at[c], p_send.at[c], p_recv.at[c], (sector, other_core)
        )

    def stack_copy(c, step):
        there = pl.ds(pl.multiple_of(lax.rem(stack + step, stacks) * part_rows, 8), part_rows)
        return send(
            half.at[c, there], part_in.at[c, step - 1], y_send.at[c, step - 1],
            y_recv.at[c, step - 1], (sector, stack_at(step)),
        )

    def part_at(c):
        first = c * rows + core * pair_rows + stack * part_rows
        return pl.ds(pl.multiple_of(first, 8), part_rows)

    def give_stack(c, step):
        here = part_at(c)
        return send(
            resid.at[here], resid.at[here], g_send.at[c, step - 1], g_recv.at[c, step - 1],
            (sector, stack_at(step)),
        )

    def give_pair(c):
        here = pl.ds(pl.multiple_of(c * rows + core * pair_rows, 8), pair_rows)
        return send(
            resid.at[here], resid.at[here], h_send.at[c], h_recv.at[c], (sector, other_core)
        )

    def apply(turn, vec_ref, out_ref):
        hi[...], lo[...] = split(vec_ref[...])
        if turn == 0:
            pl.semaphore_wait(barrier, sectors + bonds - 2)

        def make(c, carry):
            here = pl.ds(pl.multiple_of(c * rows, rows), rows)
            own[here, :] = dot_split(left_ref[here, :], hi[...], lo[...]).astype(bf16)
            start(FROM_PARTNER, c)
            if not lean:
                start(FROM_BELOW, c)
                start(FROM_ABOVE, c)
            return carry

        lax.fori_loop(0, chunks, make, 0)
        if turn == 0:
            right_hi[...], right_lo[...] = split(right_ref[...])

        def forward(c):
            arrive(FROM_PARTNER, c)
            if lean:
                here = pl.ds(pl.multiple_of(c * rows, rows), rows)
                mine = own[here, :].astype(f32)
                theirs = slots[FROM_PARTNER, here, :].astype(f32)
                for kind, take in zip((FROM_BELOW, FROM_ABOVE), takes):
                    value = mine * take + theirs * (1.0 - take)
                    pick[kind - FROM_BELOW, here, :] = value.astype(bf16)
                    start(kind, c)
            else:
                start(ABOVE_RELAY, c)
                arrive(FROM_ABOVE, c)
                start(PARTNER_RELAY, c)

        def forward_far(c):
            arrive(PARTNER_RELAY, c)
            start(BELOW_RELAY, c)

        def mix(c):
            here = pl.ds(pl.multiple_of(c * rows, rows), rows)
            for kind in (FROM_BELOW, FROM_ABOVE) if lean else (FROM_BELOW, ABOVE_RELAY, BELOW_RELAY):
                arrive(kind, c)
            mixed = own_weight * own[here, :].astype(f32)
            term[here, :] = mixed + weights[0] * slots[FROM_PARTNER, here, :].astype(f32)
            for kind in range(1, len(weights)):

                def add(kind=kind):
                    term[here, :] += weights[kind] * slots[kind, here, :].astype(f32)

                when(gets_if[kind], add)
            term[here, :] = dot_split(term[here, :], right_hi[...], right_lo[...])
            pair_copy(c).start()

        def reduce_pair(c):
            pair_copy(c).wait_recv()
            mine = pl.ds(pl.multiple_of(c * rows + core * pair_rows, 8), pair_rows)
            half[c] = term[mine, :] + half_in[c]
            for step in range(1, stacks):
                stack_copy(c, step).start()

        def reduce_stack(c):
            mine = pl.ds(pl.multiple_of(stack * part_rows, 8), part_rows)
            total = half[c, mine, :]
            for step in range(1, stacks):
                stack_copy(c, step).wait_recv()
                total = total + part_in[c, step - 1]
            here = part_at(c)
            total = total - coef_ref[turn] * vec_ref[here, :]
            if turn == 1:
                total = total - coef_ref[2] * psi_ref[here, :]
            resid[here, :] = total
            for step in range(1, stacks):
                give_stack(c, step).start()
            square = jnp.sum((total * total).reshape(part_rows // 8, 8, width), axis=0)
            folded = squares[...]
            for lane in range(0, width, 128):
                folded = folded + square[:, lane : lane + 128]
            squares[...] = folded

            @pl.when(c == chunks - 1)
            def _():
                parts[turn, bond] = squares[...]
                for step in range(1, bonds):
                    part_copy(step).start()

        def part_copy(step):
            return send(
                parts.at[turn, bond], parts.at[turn, bond],
                q_send.at[turn, step - 1], q_recv.at[turn, step - 1],
                (sector, lax.rem(bond + step, bonds)),
            )

        def gather_pair(c):
            for step in range(1, stacks):
                give_stack(c, step).wait_recv()
            give_pair(c).start()

        stages = [forward] + ([] if lean else [forward_far])
        stages += [mix, reduce_pair, reduce_stack, gather_pair]

        def advance(c, carry):
            for late, action in enumerate(stages):
                pl.when((c >= late) & (c < chunks + late))(
                    functools.partial(action, c - late)
                )
            return carry

        squares[...] = jnp.zeros_like(squares)
        lax.fori_loop(0, chunks + len(stages) - 1, advance, 0)

        for step in range(1, bonds):
            part_copy(step).wait_recv()
        sums[turn, sector] = jnp.sum(parts[turn], axis=0)

        def sum_copy(step):
            return send(
                sums.at[turn, sector], sums.at[turn, sector],
                s_send.at[turn, step - 1], s_recv.at[turn, step - 1],
                (lax.rem(sector + step, sectors), bond),
            )

        for c in range(chunks):
            for kind in range(len(weights)):
                when(sends_if[kind], lambda kind=kind: block_copy(kind, c).wait_send())
        for step in range(1, sectors):
            sum_copy(step).start()
        for step in range(1, bonds):
            part_copy(step).wait_send()
        for c in range(chunks):
            give_pair(c).wait_recv()
            pair_copy(c).wait_send()
            for step in range(1, stacks):
                stack_copy(c, step).wait_send()
                give_stack(c, step).wait_send()
            give_pair(c).wait_send()
        for step in range(1, sectors):
            sum_copy(step).wait_recv()
        total = jnp.sum(sums[turn], axis=0)
        total = jnp.sum(jnp.sum(total, axis=0, keepdims=True), axis=1, keepdims=True)
        scale = 1.0 / jnp.sqrt(total / cells + EPS)
        for c in range(chunks):
            here = pl.ds(c * rows, rows)
            out_ref[here, :] = resid[here, :] * scale
        for step in range(1, sectors):
            sum_copy(step).wait_send()

    apply(0, psi_ref, one_ref)
    apply(1, one_ref, two_ref)


def both(lean, sectors, bonds, operands):
    width = operands[-1].shape[0]
    chunks = FULL_CHUNKS
    kinds = 3 if lean else 6
    rows = width // chunks
    far = max(bonds // 2 - 1, 1)
    dma = pltpu.SemaphoreType.DMA
    smem = pl.BlockSpec(memory_space=pltpu.SMEM)
    vmem = pl.BlockSpec(memory_space=pltpu.VMEM)
    cells = float(sectors * width * width)
    block = jax.ShapeDtypeStruct((width, width), f32)
    half_block = pltpu.VMEM((width, width), bf16)
    return pl.pallas_call(
        functools.partial(kernel, lean, chunks, sectors, bonds, cells),
        out_shape=(block, block),
        in_specs=[smem] * 5 + [vmem] * 3,
        out_specs=(vmem, vmem),
        scratch_shapes=[
            half_block, half_block, half_block, half_block, half_block,
            pltpu.VMEM((2, width, width) if lean else (1, 16, 128), bf16),
            pltpu.VMEM((kinds, width, width), bf16),
            pltpu.VMEM((width, width), f32),
            pltpu.VMEM((chunks, rows // 2, width), f32),
            pltpu.VMEM((chunks, rows // 2, width), f32),
            pltpu.VMEM((chunks, far, rows // bonds, width), f32),
            pltpu.VMEM((width, width), f32),
            pltpu.VMEM((8, 128), f32),
            pltpu.VMEM((2, bonds, 8, 128), f32),
            pltpu.VMEM((2, sectors, 8, 128), f32),
            dma((kinds, chunks)), dma((kinds, chunks)),
            dma((chunks,)), dma((chunks,)),
            dma((chunks, far)), dma((chunks, far)),
            dma((chunks, far)), dma((chunks, far)),
            dma((chunks,)), dma((chunks,)),
            dma((2, bonds - 1)), dma((2, bonds - 1)),
            dma((2, sectors - 1)), dma((2, sectors - 1)),
        ],
        compiler_params=pltpu.CompilerParams(
            collective_id=int(lean), has_side_effects=True, vmem_limit_bytes=60 * 2**20
        ),
        name="lean" if lean else "full",
    )(*operands)


def lean_kernel(
    chunks, sectors, bonds, cells,
    label_ref, step_ref, index_ref, entry_ref, coef_ref, left_hbm, right_hbm, psi_hbm,
    one_ref, two_ref,
    left, right, psi, hi, lo, right_hi, right_lo, own, pick, slots, term, half_in, parts, resid, squares, sums,
    in_sem, x_send, x_recv, p_send, p_recv, y_send, y_recv, h_send, h_recv, s_send, s_recv,
):
    sector, bond = lax.axis_index("sector"), lax.axis_index("mpo")
    width = left.shape[0]
    rows = width // chunks
    pair_rows = rows // 2
    stacks = bonds // 2
    core, stack = lax.rem(bond, 2), bond // 2
    sign = 1 - 2 * lax.rem(sector, 2)
    partner, ahead, behind = sector + sign, sector + 2 * sign, sector - 2 * sign
    has_ahead = (ahead >= 0) & (ahead < sectors)
    has_behind = (behind >= 0) & (behind < sectors)
    other_core = stack * 2 + 1 - core
    entries = step_ref.shape[0]
    peers = sectors * 2
    me = sector * 2 + core

    def peer_at(step):
        peer = lax.rem(me + step, peers)
        return (peer // 2, stack * 2 + lax.rem(peer, 2))

    def stack_at(step):
        return (sector, lax.rem(stack + step, stacks) * 2 + core)

    load_rows = width // LOADS

    def load(which, n):
        source, target = ((psi_hbm, psi), (left_hbm, left), (right_hbm, right))[which]
        here = pl.ds(n * load_rows, load_rows)
        return pltpu.make_async_copy(source.at[here], target.at[here], in_sem.at[which, n])

    for which in range(3):
        for n in range(LOADS):
            load(which, n).start()

    barrier = pltpu.get_barrier_semaphore()
    for step in range(1, peers):
        pl.semaphore_signal(barrier, inc=1, device_id=peer_at(step), device_id_type=MESH)
    for step in range(1, stacks):
        pl.semaphore_signal(barrier, inc=1, device_id=stack_at(step), device_id_type=MESH)

    def inside(slot):
        return jnp.minimum(jnp.maximum(slot, 0), sectors - 1)

    own_label = label_ref[sector]

    def couple(source):
        slot = inside(source)
        label = label_ref[slot]
        total = f32(0.0)
        for entry in range(entries):
            match = label + step_ref[entry, bond, slot] == own_label
            value = entry_ref[index_ref[entry, bond, slot]]
            total = total + jnp.where(match, value, f32(0.0))
        return jnp.where(source == slot, total, f32(0.0))

    def adjacent(slot):
        gap = label_ref[inside(slot)] - own_label
        return (gap == 1) | (gap == -1)

    takes = (jnp.where(adjacent(ahead), f32(1.0), f32(0.0)),
             jnp.where(adjacent(behind), f32(1.0), f32(0.0)))
    own_weight = couple(sector)
    weights = (
        couple(partner),
        jnp.where(adjacent(behind), couple(behind), couple(behind + sign)),
        jnp.where(adjacent(ahead), couple(ahead), couple(ahead + sign)),
    )

    def send(source, target, send_sem, recv_sem, device):
        return pltpu.make_async_remote_copy(
            src_ref=source, dst_ref=target, send_sem=send_sem, recv_sem=recv_sem,
            device_id=device, device_id_type=MESH,
        )

    def rows_at(c):
        return pl.ds(pl.multiple_of(c * rows, rows), rows)

    def block_copy(kind, c):
        here = rows_at(c)
        source, device = {
            FROM_PARTNER: (own, partner),
            FROM_BELOW: (pick.at[0], ahead),
            FROM_ABOVE: (pick.at[1], behind),
        }[kind]
        return send(
            source.at[here], slots.at[kind, here], x_send.at[kind, c], x_recv.at[kind, c],
            (device, bond),
        )

    sends_if = {FROM_PARTNER: None, FROM_BELOW: has_ahead, FROM_ABOVE: has_behind}
    gets_if = {FROM_PARTNER: None, FROM_BELOW: has_behind, FROM_ABOVE: has_ahead}

    def when(condition, action):
        if condition is None:
            action()
        else:
            pl.when(condition)(action)

    def start(kind, c):
        when(sends_if[kind], lambda: block_copy(kind, c).start())

    def arrive(kind, c):
        when(gets_if[kind], lambda: block_copy(kind, c).wait_recv())

    def pair_copy(c):
        there = c * rows + (1 - core) * pair_rows
        there = pl.ds(pl.multiple_of(there, 8), pair_rows)
        return send(
            term.at[there], half_in.at[c], p_send.at[c], p_recv.at[c], (sector, other_core)
        )

    def half_at(c, which):
        return pl.ds(pl.multiple_of(c * rows + which * pair_rows, 8), pair_rows)

    def stack_copy(turn, c, step):
        here = parts.at[turn, stack, c]
        return send(here, here, y_send.at[c, step - 1], y_recv.at[c, step - 1], stack_at(step))

    def give_pair(turn, c):
        here = resid.at[turn, half_at(c, core)]
        return send(here, here, h_send.at[c], h_recv.at[c], (sector, other_core))

    def sum_copy(turn, step):
        here = sums.at[turn, me]
        return send(here, here, s_send.at[turn, step - 1], s_recv.at[turn, step - 1], peer_at(step))

    def dots(left_value, right_high, right_low):
        high, low = split(left_value)
        dot = functools.partial(jnp.dot, preferred_element_type=f32)
        count = left_value.shape[0]
        both_rows = dot(jnp.concatenate([high, low], axis=0), right_high)
        return both_rows[:count] + (both_rows[count:] + dot(high, right_low))

    def apply(turn, scale):
        def forward(c):
            here = rows_at(c)
            arrive(FROM_PARTNER, c)
            mine = own[here, :].astype(f32)
            theirs = slots[FROM_PARTNER, here, :].astype(f32)
            for kind, take in zip((FROM_BELOW, FROM_ABOVE), takes):
                value = mine * take + theirs * (1.0 - take)
                pick[kind - FROM_BELOW, here, :] = value.astype(bf16)
                start(kind, c)

        def mix(c):
            here = rows_at(c)
            arrive(FROM_BELOW, c)
            arrive(FROM_ABOVE, c)
            mixed = own_weight * own[here, :].astype(f32)
            term[here, :] = mixed + weights[0] * slots[FROM_PARTNER, here, :].astype(f32)
            for kind in (FROM_BELOW, FROM_ABOVE):

                def add(kind=kind):
                    term[here, :] += weights[kind] * slots[kind, here, :].astype(f32)

                when(gets_if[kind], add)
            term[here, :] = dots(term[here, :], right_hi[...], right_lo[...])
            pair_copy(c).start()

        def reduce_pair(c):
            pair_copy(c).wait_recv()
            parts[turn, stack, c] = term[half_at(c, core), :] + half_in[c]
            for step in range(1, stacks):
                stack_copy(turn, c, step).start()

        def reduce_stack(c):
            for step in range(1, stacks):
                stack_copy(turn, c, step).wait_recv()
            total = parts[turn, 0, c]
            for place in range(1, stacks):
                total = total + parts[turn, place, c]
            here = half_at(c, core)
            if turn == 0:
                total = total - coef_ref[0] * psi[here, :]
            else:
                total = total - coef_ref[1] * (resid[0, here, :] * scale)
                total = total - coef_ref[2] * psi[here, :]
            resid[turn, here, :] = total
            give_pair(turn, c).start()
            square = jnp.sum((total * total).reshape(pair_rows // 8, 8, width), axis=0)
            folded = squares[...]
            for lane in range(0, width, 128):
                folded = folded + square[:, lane : lane + 128]
            squares[...] = folded

            @pl.when(c == chunks - 1)
            def _():
                sums[turn, me] = jnp.sum(squares[...], axis=0, keepdims=True)
                for step in range(1, peers):
                    sum_copy(turn, step).start()

        def gather(c):
            give_pair(turn, c).wait_recv()
            if turn == 0:
                here = rows_at(c)
                hi[here, :], lo[here, :] = split(resid[0, here, :])

        stages = [(0, forward), (3, reduce_pair), (2, mix), (5, reduce_stack), (6, gather)]

        def advance(c, carry):
            for late, action in stages:
                pl.when((c >= late) & (c < chunks + late))(
                    functools.partial(action, c - late)
                )
            return carry

        squares[...] = jnp.zeros_like(squares)
        lax.fori_loop(0, chunks + max(late for late, _ in stages), advance, 0)

    def drain_sends(turn):
        def one(c, carry):
            for kind in range(3):
                when(sends_if[kind], lambda kind=kind: block_copy(kind, c).wait_send())
            pair_copy(c).wait_send()
            for step in range(1, stacks):
                stack_copy(turn, c, step).wait_send()
            give_pair(turn, c).wait_send()
            return carry

        lax.fori_loop(0, chunks, one, 0)

    def norm(turn):
        for step in range(1, peers):
            sum_copy(turn, step).wait_recv()
        total = jnp.sum(sums[turn], axis=0)
        total = jnp.sum(total, axis=1, keepdims=True)
        return 1.0 / jnp.sqrt(total / cells + EPS)

    for n in range(LOADS):
        here = pl.ds(n * load_rows, load_rows)
        load(0, n).wait()
        hi[here, :], lo[here, :] = split(psi[here, :])
    for n in range(LOADS):
        here = pl.ds(n * load_rows, load_rows)
        load(1, n).wait()
        own[here, :] = dots(left[here, :], hi[...], lo[...]).astype(bf16)
        if n == 0:
            pl.semaphore_wait(barrier, peers + stacks - 2)
        for c in range(n * load_rows // rows, (n + 1) * load_rows // rows):
            start(FROM_PARTNER, c)
    for n in range(LOADS):
        here = pl.ds(n * load_rows, load_rows)
        load(2, n).wait()
        right_hi[here, :], right_lo[here, :] = split(right[here, :])
    apply(0, None)

    drain_sends(0)
    term[...] = dot_split(left[...], hi[...], lo[...])
    scale = norm(0)

    def begin(c, carry):
        here = rows_at(c)
        own[here, :] = (term[here, :] * scale).astype(bf16)
        start(FROM_PARTNER, c)
        return carry

    lax.fori_loop(0, chunks, begin, 0)
    one_ref[...] = resid[0] * scale
    apply(1, scale)
    drain_sends(1)
    last = norm(1)
    two_ref[...] = resid[1] * last
    for turn in range(2):
        for step in range(1, peers):
            sum_copy(turn, step).wait_send()


def lean_call(sectors, bonds, operands):
    width = operands[-1].shape[0]
    chunks = LINK_CHUNKS
    rows = width // chunks
    stacks = bonds // 2
    peers = sectors * 2
    dma = pltpu.SemaphoreType.DMA
    smem = pl.BlockSpec(memory_space=pltpu.SMEM)
    vmem = pl.BlockSpec(memory_space=pltpu.VMEM)
    whole = pl.BlockSpec(memory_space=pl.ANY)
    cells = float(sectors * width * width)
    block = jax.ShapeDtypeStruct((width, width), f32)
    full_block = pltpu.VMEM((width, width), f32)
    half_block = pltpu.VMEM((width, width), bf16)
    return pl.pallas_call(
        functools.partial(lean_kernel, chunks, sectors, bonds, cells),
        out_shape=(block, block),
        in_specs=[smem] * 5 + [whole] * 3,
        out_specs=(vmem, vmem),
        scratch_shapes=[
            full_block, full_block, full_block,
            half_block, half_block, half_block, half_block, half_block,
            pltpu.VMEM((2, width, width), bf16),
            pltpu.VMEM((3, width, width), bf16),
            full_block,
            pltpu.VMEM((chunks, rows // 2, width), f32),
            pltpu.VMEM((2, stacks, chunks, rows // 2, width), f32),
            pltpu.VMEM((2, width, width), f32),
            pltpu.VMEM((8, 128), f32),
            pltpu.VMEM((2, peers, 1, 128), f32),
            dma((3, LOADS)),
            dma((3, chunks)), dma((3, chunks)),
            dma((chunks,)), dma((chunks,)),
            dma((chunks, stacks - 1)), dma((chunks, stacks - 1)),
            dma((chunks,)), dma((chunks,)),
            dma((2, peers - 1)), dma((2, peers - 1)),
        ],
        compiler_params=pltpu.CompilerParams(
            collective_id=1, has_side_effects=True, vmem_limit_bytes=48 * 2**20
        ),
        name="lean",
    )(*operands)


def one_block_per_plane(sector_label):
    sectors = sector_label.shape[0]
    plane = jnp.arange(sectors, dtype=jnp.int32) // 2
    upward = sector_label // 2 - plane
    downward = (sectors - 1 - sector_label) // 2 - plane
    misses = jnp.sum(jnp.abs(upward) + (jnp.abs(downward) << 16))
    return ((misses & 0xFFFF) == 0) | ((misses >> 16) == 0)


def local(
    sectors, bonds,
    psi, left_env, right_env, sector_label, charge_step, coef_index, entry_values, recurrence,
):
    operands = (
        sector_label, charge_step.transpose(2, 0, 1), coef_index.transpose(2, 0, 1), entry_values, recurrence,
        left_env[0, 0], right_env[0, 0], psi[0],
    )
    vec_one, vec_two = lax.cond(
        one_block_per_plane(sector_label),
        lambda: lean_call(sectors, bonds, operands),
        lambda: both(False, sectors, bonds, operands),
    )
    return (vec_one[None], vec_two[None])


def solution(mesh):
    in_specs = (
        P("sector", None, None),
        P("mpo", "sector", None, None),
        P("mpo", "sector", None, None),
        P(),
        P(),
        P(),
        P(),
        P(),
    )
    out_specs = (P("sector", None, None), P("sector", None, None))
    body = functools.partial(local, mesh.shape["sector"], mesh.shape["mpo"])
    return jax.shard_map(body, mesh=mesh, in_specs=in_specs, out_specs=out_specs, check_vma=False)
```

```python
import functools

import jax
import jax.numpy as jnp
from jax import lax
from jax.experimental import pallas as pl
from jax.experimental.pallas import tpu as pltpu
from jax.sharding import PartitionSpec as P

EPS = 1e-06
LINK_CHUNKS, FULL_CHUNKS, LOADS = 16, 3, 4
FROM_PARTNER, FROM_BELOW, FROM_ABOVE, PARTNER_RELAY, ABOVE_RELAY, BELOW_RELAY = range(6)
MESH = pl.DeviceIdType.MESH
f32, bf16 = jnp.float32, jnp.bfloat16


def split(value):
    high = value.astype(bf16)
    return high, (value - high.astype(f32)).astype(bf16)


def dot_split(left, right_high, right_low):
    high, low = split(left)
    dot = functools.partial(jnp.dot, preferred_element_type=f32)
    return dot(high, right_high) + (dot(low, right_high) + dot(high, right_low))


def kernel(
    lean, chunks, sectors, bonds, cells,
    label_ref, step_ref, index_ref, entry_ref, coef_ref, left_ref, right_ref, psi_ref,
    one_ref, two_ref,
    hi, lo, right_hi, right_lo, own, pick, slots, term, half_in, half, part_in, resid, squares, parts, sums,
    x_send, x_recv, p_send, p_recv, y_send, y_recv, g_send, g_recv, h_send, h_recv, q_send, q_recv, s_send, s_recv,
):
    sector, bond = lax.axis_index("sector"), lax.axis_index("mpo")
    width = left_ref.shape[0]
    rows = width // chunks
    pair_rows = rows // 2
    stacks = bonds // 2
    part_rows = pair_rows // stacks
    core, stack = lax.rem(bond, 2), bond // 2
    sign = 1 - 2 * lax.rem(sector, 2)
    partner, ahead, behind = sector + sign, sector + 2 * sign, sector - 2 * sign
    has_ahead = (ahead >= 0) & (ahead < sectors)
    has_behind = (behind >= 0) & (behind < sectors)
    has_far = (sector - 4 * sign >= 0) & (sector - 4 * sign < sectors)
    other_core = stack * 2 + 1 - core
    entries = step_ref.shape[0]

    def stack_at(step):
        return lax.rem(stack + step, stacks) * 2 + core

    barrier = pltpu.get_barrier_semaphore()
    for step in range(1, sectors):
        pl.semaphore_signal(
            barrier, inc=1, device_id=(lax.rem(sector + step, sectors), bond), device_id_type=MESH
        )
    for step in range(1, bonds):
        pl.semaphore_signal(
            barrier, inc=1, device_id=(sector, lax.rem(bond + step, bonds)), device_id_type=MESH
        )

    def inside(slot):
        return jnp.minimum(jnp.maximum(slot, 0), sectors - 1)

    own_label = label_ref[sector]

    def couple(source):
        slot = inside(source)
        label = label_ref[slot]
        total = f32(0.0)
        for entry in range(entries):
            match = label + step_ref[entry, bond, slot] == own_label
            value = entry_ref[index_ref[entry, bond, slot]]
            total = total + jnp.where(match, value, f32(0.0))
        return jnp.where(source == slot, total, f32(0.0))

    def adjacent(slot):
        gap = label_ref[inside(slot)] - own_label
        return (gap == 1) | (gap == -1)

    own_weight = couple(sector)
    if lean:
        takes = (jnp.where(adjacent(ahead), f32(1.0), f32(0.0)),
                 jnp.where(adjacent(behind), f32(1.0), f32(0.0)))
        weights = (
            couple(partner),
            jnp.where(adjacent(behind), couple(behind), couple(behind + sign)),
            jnp.where(adjacent(ahead), couple(ahead), couple(ahead + sign)),
        )
    else:
        weights = tuple(couple(sector + sign * place) for place in (1, -2, 2, -1, 3, -3))

    def send(source, target, send_sem, recv_sem, device):
        return pltpu.make_async_remote_copy(
            src_ref=source, dst_ref=target, send_sem=send_sem, recv_sem=recv_sem,
            device_id=device, device_id_type=MESH,
        )

    def block_copy(kind, c):
        here = pl.ds(pl.multiple_of(c * rows, rows), rows)
        source, device = {
            FROM_PARTNER: (own, partner),
            FROM_BELOW: (pick.at[0] if lean else own, ahead),
            FROM_ABOVE: (pick.at[1] if lean else own, behind),
            PARTNER_RELAY: (slots.at[FROM_ABOVE], partner),
            ABOVE_RELAY: (slots.at[FROM_PARTNER], behind),
            BELOW_RELAY: (slots.at[min(PARTNER_RELAY, len(weights) - 1)], ahead),
        }[kind]
        return send(
            source.at[here], slots.at[kind, here], x_send.at[kind, c], x_recv.at[kind, c],
            (device, bond),
        )

    sends_if = {
        FROM_PARTNER: None, FROM_BELOW: has_ahead, FROM_ABOVE: has_behind,
        PARTNER_RELAY: has_ahead, ABOVE_RELAY: has_behind, BELOW_RELAY: has_ahead & has_behind,
    }
    gets_if = {
        FROM_PARTNER: None, FROM_BELOW: has_behind, FROM_ABOVE: has_ahead,
        PARTNER_RELAY: has_behind, ABOVE_RELAY: has_ahead, BELOW_RELAY: has_far,
    }

    def when(condition, action):
        if condition is None:
            action()
        else:
            pl.when(condition)(action)

    def start(kind, c):
        when(sends_if[kind], lambda: block_copy(kind, c).start())

    def arrive(kind, c):
        when(gets_if[kind], lambda: block_copy(kind, c).wait_recv())

    def pair_copy(c):
        there = c * rows + (1 - core) * pair_rows
        there = pl.ds(pl.multiple_of(there, 8), pair_rows)
        return send(
            term.at[there], half_in.at[c], p_send.at[c], p_recv.at[c], (sector, other_core)
        )

    def stack_copy(c, step):
        there = pl.ds(pl.multiple_of(lax.rem(stack + step, stacks) * part_rows, 8), part_rows)
        return send(
            half.at[c, there], part_in.at[c, step - 1], y_send.at[c, step - 1],
            y_recv.at[c, step - 1], (sector, stack_at(step)),
        )

    def part_at(c):
        first = c * rows + core * pair_rows + stack * part_rows
        return pl.ds(pl.multiple_of(first, 8), part_rows)

    def give_stack(c, step):
        here = part_at(c)
        return send(
            resid.at[here], resid.at[here], g_send.at[c, step - 1], g_recv.at[c, step - 1],
            (sector, stack_at(step)),
        )

    def give_pair(c):
        here = pl.ds(pl.multiple_of(c * rows + core * pair_rows, 8), pair_rows)
        return send(
            resid.at[here], resid.at[here], h_send.at[c], h_recv.at[c], (sector, other_core)
        )

    def apply(turn, vec_ref, out_ref):
        hi[...], lo[...] = split(vec_ref[...])
        if turn == 0:
            pl.semaphore_wait(barrier, sectors + bonds - 2)

        def make(c, carry):
            here = pl.ds(pl.multiple_of(c * rows, rows), rows)
            own[here, :] = dot_split(left_ref[here, :], hi[...], lo[...]).astype(bf16)
            start(FROM_PARTNER, c)
            if not lean:
                start(FROM_BELOW, c)
                start(FROM_ABOVE, c)
            return carry

        lax.fori_loop(0, chunks, make, 0)
        if turn == 0:
            right_hi[...], right_lo[...] = split(right_ref[...])

        def forward(c):
            arrive(FROM_PARTNER, c)
            if lean:
                here = pl.ds(pl.multiple_of(c * rows, rows), rows)
                mine = own[here, :].astype(f32)
                theirs = slots[FROM_PARTNER, here, :].astype(f32)
                for kind, take in zip((FROM_BELOW, FROM_ABOVE), takes):
                    value = mine * take + theirs * (1.0 - take)
                    pick[kind - FROM_BELOW, here, :] = value.astype(bf16)
                    start(kind, c)
            else:
                start(ABOVE_RELAY, c)
                arrive(FROM_ABOVE, c)
                start(PARTNER_RELAY, c)

        def forward_far(c):
            arrive(PARTNER_RELAY, c)
            start(BELOW_RELAY, c)

        def mix(c):
            here = pl.ds(pl.multiple_of(c * rows, rows), rows)
            for kind in (FROM_BELOW, FROM_ABOVE) if lean else (FROM_BELOW, ABOVE_RELAY, BELOW_RELAY):
                arrive(kind, c)
            mixed = own_weight * own[here, :].astype(f32)
            term[here, :] = mixed + weights[0] * slots[FROM_PARTNER, here, :].astype(f32)
            for kind in range(1, len(weights)):

                def add(kind=kind):
                    term[here, :] += weights[kind] * slots[kind, here, :].astype(f32)

                when(gets_if[kind], add)
            term[here, :] = dot_split(term[here, :], right_hi[...], right_lo[...])
            pair_copy(c).start()

        def reduce_pair(c):
            pair_copy(c).wait_recv()
            mine = pl.ds(pl.multiple_of(c * rows + core * pair_rows, 8), pair_rows)
            half[c] = term[mine, :] + half_in[c]
            for step in range(1, stacks):
                stack_copy(c, step).start()

        def reduce_stack(c):
            mine = pl.ds(pl.multiple_of(stack * part_rows, 8), part_rows)
            total = half[c, mine, :]
            for step in range(1, stacks):
                stack_copy(c, step).wait_recv()
                total = total + part_in[c, step - 1]
            here = part_at(c)
            total = total - coef_ref[turn] * vec_ref[here, :]
            if turn == 1:
                total = total - coef_ref[2] * psi_ref[here, :]
            resid[here, :] = total
            for step in range(1, stacks):
                give_stack(c, step).start()
            square = jnp.sum((total * total).reshape(part_rows // 8, 8, width), axis=0)
            folded = squares[...]
            for lane in range(0, width, 128):
                folded = folded + square[:, lane : lane + 128]
            squares[...] = folded

            @pl.when(c == chunks - 1)
            def _():
                parts[turn, bond] = squares[...]
                for step in range(1, bonds):
                    part_copy(step).start()

        def part_copy(step):
            return send(
                parts.at[turn, bond], parts.at[turn, bond],
                q_send.at[turn, step - 1], q_recv.at[turn, step - 1],
                (sector, lax.rem(bond + step, bonds)),
            )

        def gather_pair(c):
            for step in range(1, stacks):
                give_stack(c, step).wait_recv()
            give_pair(c).start()

        stages = [forward] + ([] if lean else [forward_far])
        stages += [mix, reduce_pair, reduce_stack, gather_pair]

        def advance(c, carry):
            for late, action in enumerate(stages):
                pl.when((c >= late) & (c < chunks + late))(
                    functools.partial(action, c - late)
                )
            return carry

        squares[...] = jnp.zeros_like(squares)
        lax.fori_loop(0, chunks + len(stages) - 1, advance, 0)

        for step in range(1, bonds):
            part_copy(step).wait_recv()
        sums[turn, sector] = jnp.sum(parts[turn], axis=0)

        def sum_copy(step):
            return send(
                sums.at[turn, sector], sums.at[turn, sector],
                s_send.at[turn, step - 1], s_recv.at[turn, step - 1],
                (lax.rem(sector + step, sectors), bond),
            )

        for c in range(chunks):
            for kind in range(len(weights)):
                when(sends_if[kind], lambda kind=kind: block_copy(kind, c).wait_send())
        for step in range(1, sectors):
            sum_copy(step).start()
        for step in range(1, bonds):
            part_copy(step).wait_send()
        for c in range(chunks):
            give_pair(c).wait_recv()
            pair_copy(c).wait_send()
            for step in range(1, stacks):
                stack_copy(c, step).wait_send()
                give_stack(c, step).wait_send()
            give_pair(c).wait_send()
        for step in range(1, sectors):
            sum_copy(step).wait_recv()
        total = jnp.sum(sums[turn], axis=0)
        total = jnp.sum(jnp.sum(total, axis=0, keepdims=True), axis=1, keepdims=True)
        scale = 1.0 / jnp.sqrt(total / cells + EPS)
        for c in range(chunks):
            here = pl.ds(c * rows, rows)
            out_ref[here, :] = resid[here, :] * scale
        for step in range(1, sectors):
            sum_copy(step).wait_send()

    apply(0, psi_ref, one_ref)
    apply(1, one_ref, two_ref)


def both(lean, sectors, bonds, operands):
    width = operands[-1].shape[0]
    chunks = FULL_CHUNKS
    kinds = 3 if lean else 6
    rows = width // chunks
    far = max(bonds // 2 - 1, 1)
    dma = pltpu.SemaphoreType.DMA
    smem = pl.BlockSpec(memory_space=pltpu.SMEM)
    vmem = pl.BlockSpec(memory_space=pltpu.VMEM)
    cells = float(sectors * width * width)
    block = jax.ShapeDtypeStruct((width, width), f32)
    half_block = pltpu.VMEM((width, width), bf16)
    return pl.pallas_call(
        functools.partial(kernel, lean, chunks, sectors, bonds, cells),
        out_shape=(block, block),
        in_specs=[smem] * 5 + [vmem] * 3,
        out_specs=(vmem, vmem),
        scratch_shapes=[
            half_block, half_block, half_block, half_block, half_block,
            pltpu.VMEM((2, width, width) if lean else (1, 16, 128), bf16),
            pltpu.VMEM((kinds, width, width), bf16),
            pltpu.VMEM((width, width), f32),
            pltpu.VMEM((chunks, rows // 2, width), f32),
            pltpu.VMEM((chunks, rows // 2, width), f32),
            pltpu.VMEM((chunks, far, rows // bonds, width), f32),
            pltpu.VMEM((width, width), f32),
            pltpu.VMEM((8, 128), f32),
            pltpu.VMEM((2, bonds, 8, 128), f32),
            pltpu.VMEM((2, sectors, 8, 128), f32),
            dma((kinds, chunks)), dma((kinds, chunks)),
            dma((chunks,)), dma((chunks,)),
            dma((chunks, far)), dma((chunks, far)),
            dma((chunks, far)), dma((chunks, far)),
            dma((chunks,)), dma((chunks,)),
            dma((2, bonds - 1)), dma((2, bonds - 1)),
            dma((2, sectors - 1)), dma((2, sectors - 1)),
        ],
        compiler_params=pltpu.CompilerParams(
            collective_id=int(lean), has_side_effects=True, vmem_limit_bytes=42 * 2**20
        ),
        name="lean" if lean else "full",
    )(*operands)


def lean_kernel(
    chunks, sectors, bonds, cells,
    label_hbm, step_hbm, index_hbm, entry_hbm, coef_hbm, left_hbm, right_hbm, psi_hbm,
    one_ref, two_ref,
    label_ref, step_ref, index_ref, entry_ref, coef_ref, left, right, psi, hi, lo, right_hi, right_lo, own, pick, slots, term, half_in, parts, resid, squares, sums,
    in_sem, small_sem, x_send, x_recv, p_send, p_recv, y_send, y_recv, h_send, h_recv, s_send, s_recv,
):
    sector, bond = lax.axis_index("sector"), lax.axis_index("mpo")
    width = left.shape[0]
    rows = width // chunks
    pair_rows = rows // 2
    stacks = bonds // 2
    core, stack = lax.rem(bond, 2), bond // 2
    sign = 1 - 2 * lax.rem(sector, 2)
    partner, ahead, behind = sector + sign, sector + 2 * sign, sector - 2 * sign
    has_ahead = (ahead >= 0) & (ahead < sectors)
    has_behind = (behind >= 0) & (behind < sectors)
    other_core = stack * 2 + 1 - core
    entries = step_ref.shape[0]
    peers = sectors * 2
    me = sector * 2 + core

    def peer_at(step):
        peer = lax.rem(me + step, peers)
        return (peer // 2, stack * 2 + lax.rem(peer, 2))

    def stack_at(step):
        return (sector, lax.rem(stack + step, stacks) * 2 + core)

    load_rows = width // LOADS

    def load(which, n):
        source, target = ((psi_hbm, psi), (left_hbm, left), (right_hbm, right))[which]
        here = pl.ds(n * load_rows, load_rows)
        return pltpu.make_async_copy(source.at[here], target.at[here], in_sem.at[which, n])

    for which in range(3):
        for n in range(LOADS):
            load(which, n).start()

    smalls = [
        pltpu.make_async_copy(source, target, small_sem.at[n])
        for n, (source, target) in enumerate((
            (label_hbm, label_ref), (step_hbm, step_ref), (index_hbm, index_ref),
            (entry_hbm, entry_ref), (coef_hbm, coef_ref),
        ))
    ]
    for small in smalls:
        small.start()
    barrier = pltpu.get_barrier_semaphore()

    def greet(device):
        pl.semaphore_signal(barrier, inc=1, device_id=device, device_id_type=MESH)

    greet((partner, bond))
    greet((sector, other_core))
    for step in range(1, stacks):
        greet(stack_at(step))
    pl.when(has_ahead)(lambda: greet((ahead, bond)))
    pl.when(has_behind)(lambda: greet((behind, bond)))
    greetings = 1 + stacks + has_ahead.astype(jnp.int32) + has_behind.astype(jnp.int32)

    def inside(slot):
        return jnp.minimum(jnp.maximum(slot, 0), sectors - 1)

    def send(source, target, send_sem, recv_sem, device):
        return pltpu.make_async_remote_copy(
            src_ref=source, dst_ref=target, send_sem=send_sem, recv_sem=recv_sem,
            device_id=device, device_id_type=MESH,
        )

    def rows_at(c):
        return pl.ds(pl.multiple_of(c * rows, rows), rows)

    def block_copy(kind, c):
        here = rows_at(c)
        source, device = {
            FROM_PARTNER: (own, partner),
            FROM_BELOW: (pick.at[0], ahead),
            FROM_ABOVE: (pick.at[1], behind),
        }[kind]
        return send(
            source.at[here], slots.at[kind, here], x_send.at[kind, c], x_recv.at[kind, c],
            (device, bond),
        )

    sends_if = {FROM_PARTNER: None, FROM_BELOW: has_ahead, FROM_ABOVE: has_behind}
    gets_if = {FROM_PARTNER: None, FROM_BELOW: has_behind, FROM_ABOVE: has_ahead}

    def when(condition, action):
        if condition is None:
            action()
        else:
            pl.when(condition)(action)

    def start(kind, c):
        when(sends_if[kind], lambda: block_copy(kind, c).start())

    def arrive(kind, c):
        when(gets_if[kind], lambda: block_copy(kind, c).wait_recv())

    def pair_copy(c):
        there = c * rows + (1 - core) * pair_rows
        there = pl.ds(pl.multiple_of(there, 8), pair_rows)
        return send(
            term.at[there], half_in.at[c], p_send.at[c], p_recv.at[c], (sector, other_core)
        )

    def half_at(c, which):
        return pl.ds(pl.multiple_of(c * rows + which * pair_rows, 8), pair_rows)

    def stack_copy(turn, c, step):
        here = parts.at[turn, stack, c]
        return send(here, here, y_send.at[c, step - 1], y_recv.at[c, step - 1], stack_at(step))

    def give_pair(turn, c):
        here = resid.at[turn, half_at(c, core)]
        return send(here, here, h_send.at[c], h_recv.at[c], (sector, other_core))

    def sum_copy(turn, step):
        here = sums.at[turn, me]
        return send(here, here, s_send.at[turn, step - 1], s_recv.at[turn, step - 1], peer_at(step))

    def dots(left_value, right_high, right_low):
        high, low = split(left_value)
        dot = functools.partial(jnp.dot, preferred_element_type=f32)
        count = left_value.shape[0]
        both_rows = dot(jnp.concatenate([high, low], axis=0), right_high)
        return both_rows[:count] + (both_rows[count:] + dot(high, right_low))

    def apply(turn, scale):
        def forward(c):
            here = rows_at(c)
            arrive(FROM_PARTNER, c)
            mine = own[here, :].astype(f32)
            theirs = slots[FROM_PARTNER, here, :].astype(f32)
            for kind, take in zip((FROM_BELOW, FROM_ABOVE), takes):
                value = mine * take + theirs * (1.0 - take)
                pick[kind - FROM_BELOW, here, :] = value.astype(bf16)
                start(kind, c)

        def mix(c):
            here = rows_at(c)
            arrive(FROM_BELOW, c)
            arrive(FROM_ABOVE, c)
            mixed = own_weight * own[here, :].astype(f32)
            term[here, :] = mixed + weights[0] * slots[FROM_PARTNER, here, :].astype(f32)
            for kind in (FROM_BELOW, FROM_ABOVE):

                def add(kind=kind):
                    term[here, :] += weights[kind] * slots[kind, here, :].astype(f32)

                when(gets_if[kind], add)
            term[here, :] = dots(term[here, :], right_hi[...], right_lo[...])
            pair_copy(c).start()

        def reduce_pair(c):
            pair_copy(c).wait_recv()
            parts[turn, stack, c] = term[half_at(c, core), :] + half_in[c]
            for step in range(1, stacks):
                stack_copy(turn, c, step).start()

        def reduce_stack(c):
            for step in range(1, stacks):
                stack_copy(turn, c, step).wait_recv()
            total = parts[turn, 0, c]
            for place in range(1, stacks):
                total = total + parts[turn, place, c]
            here = half_at(c, core)
            if turn == 0:
                total = total - coef_ref[0] * psi[here, :]
            else:
                total = total - coef_ref[1] * (resid[0, here, :] * scale)
                total = total - coef_ref[2] * psi[here, :]
            resid[turn, here, :] = total
            give_pair(turn, c).start()
            square = jnp.sum((total * total).reshape(pair_rows // 8, 8, width), axis=0)
            folded = squares[...]
            for lane in range(0, width, 128):
                folded = folded + square[:, lane : lane + 128]
            squares[...] = folded

            @pl.when(c == chunks - 1)
            def _():
                sums[turn, me] = jnp.sum(squares[...], axis=0, keepdims=True)
                for step in range(1, peers):
                    sum_copy(turn, step).start()

        def gather(c):
            give_pair(turn, c).wait_recv()
            if turn == 0:
                here = rows_at(c)
                hi[here, :], lo[here, :] = split(resid[0, here, :])

        stages = [(0, forward), (3, reduce_pair), (2, mix), (5, reduce_stack), (6, gather)]

        def advance(c, carry):
            for late, action in stages:
                pl.when((c >= late) & (c < chunks + late))(
                    functools.partial(action, c - late)
                )
            return carry

        squares[...] = jnp.zeros_like(squares)
        lax.fori_loop(0, chunks + max(late for late, _ in stages), advance, 0)

    def drain_sends(turn):
        def one(c, carry):
            for kind in range(3):
                when(sends_if[kind], lambda kind=kind: block_copy(kind, c).wait_send())
            pair_copy(c).wait_send()
            for step in range(1, stacks):
                stack_copy(turn, c, step).wait_send()
            give_pair(turn, c).wait_send()
            return carry

        lax.fori_loop(0, chunks, one, 0)

    def norm(turn):
        for step in range(1, peers):
            sum_copy(turn, step).wait_recv()
        total = jnp.sum(sums[turn], axis=0)
        total = jnp.sum(total, axis=1, keepdims=True)
        return 1.0 / jnp.sqrt(total / cells + EPS)

    for n in range(LOADS):
        here = pl.ds(n * load_rows, load_rows)
        load(0, n).wait()
        hi[here, :], lo[here, :] = split(psi[here, :])
    for n in range(LOADS):
        here = pl.ds(n * load_rows, load_rows)
        load(1, n).wait()
        own[here, :] = dots(left[here, :], hi[...], lo[...]).astype(bf16)
        if n == 0:
            pl.semaphore_wait(barrier, greetings)
        for c in range(n * load_rows // rows, (n + 1) * load_rows // rows):
            start(FROM_PARTNER, c)
    for n in range(LOADS):
        here = pl.ds(n * load_rows, load_rows)
        load(2, n).wait()
        right_hi[here, :], right_lo[here, :] = split(right[here, :])
    for small in smalls:
        small.wait()
    own_label = label_ref[sector]

    def couple(source):
        slot = inside(source)
        label = label_ref[slot]
        total = f32(0.0)
        for entry in range(entries):
            match = label + step_ref[entry, bond, slot] == own_label
            value = entry_ref[index_ref[entry, bond, slot]]
            total = total + jnp.where(match, value, f32(0.0))
        return jnp.where(source == slot, total, f32(0.0))

    def adjacent(slot):
        gap = label_ref[inside(slot)] - own_label
        return (gap == 1) | (gap == -1)

    takes = (jnp.where(adjacent(ahead), f32(1.0), f32(0.0)),
             jnp.where(adjacent(behind), f32(1.0), f32(0.0)))
    own_weight = couple(sector)
    weights = (
        couple(partner),
        jnp.where(adjacent(behind), couple(behind), couple(behind + sign)),
        jnp.where(adjacent(ahead), couple(ahead), couple(ahead + sign)),
    )

    apply(0, None)

    drain_sends(0)
    term[...] = dot_split(left[...], hi[...], lo[...])
    scale = norm(0)

    def begin(c, carry):
        here = rows_at(c)
        own[here, :] = (term[here, :] * scale).astype(bf16)
        start(FROM_PARTNER, c)
        return carry

    lax.fori_loop(0, chunks, begin, 0)
    one_ref[...] = resid[0] * scale
    apply(1, scale)
    drain_sends(1)
    last = norm(1)
    two_ref[...] = resid[1] * last
    for turn in range(2):
        for step in range(1, peers):
            sum_copy(turn, step).wait_send()


def lean_call(sectors, bonds, operands):
    width = operands[-1].shape[0]
    chunks = LINK_CHUNKS
    rows = width // chunks
    stacks = bonds // 2
    peers = sectors * 2
    dma = pltpu.SemaphoreType.DMA
    vmem = pl.BlockSpec(memory_space=pltpu.VMEM)
    whole = pl.BlockSpec(memory_space=pl.ANY)
    cells = float(sectors * width * width)
    block = jax.ShapeDtypeStruct((width, width), f32)
    full_block = pltpu.VMEM((width, width), f32)
    half_block = pltpu.VMEM((width, width), bf16)
    return pl.pallas_call(
        functools.partial(lean_kernel, chunks, sectors, bonds, cells),
        out_shape=(block, block),
        in_specs=[whole] * 8,
        out_specs=(vmem, vmem),
        scratch_shapes=[
            *(pltpu.SMEM(small.shape, small.dtype) for small in operands[:5]),
            full_block, full_block, full_block,
            half_block, half_block, half_block, half_block, half_block,
            pltpu.VMEM((2, width, width), bf16),
            pltpu.VMEM((3, width, width), bf16),
            full_block,
            pltpu.VMEM((chunks, rows // 2, width), f32),
            pltpu.VMEM((2, stacks, chunks, rows // 2, width), f32),
            pltpu.VMEM((2, width, width), f32),
            pltpu.VMEM((8, 128), f32),
            pltpu.VMEM((2, peers, 1, 128), f32),
            dma((3, LOADS)), dma((5,)),
            dma((3, chunks)), dma((3, chunks)),
            dma((chunks,)), dma((chunks,)),
            dma((chunks, stacks - 1)), dma((chunks, stacks - 1)),
            dma((chunks,)), dma((chunks,)),
            dma((2, peers - 1)), dma((2, peers - 1)),
        ],
        compiler_params=pltpu.CompilerParams(
            collective_id=1, has_side_effects=True, vmem_limit_bytes=42 * 2**20
        ),
        name="lean",
    )(*operands)


def one_block_per_plane(sector_label):
    sectors = sector_label.shape[0]
    plane = jnp.arange(sectors, dtype=jnp.int32) // 2
    upward = sector_label // 2 - plane
    downward = (sectors - 1 - sector_label) // 2 - plane
    misses = jnp.sum(jnp.abs(upward) + (jnp.abs(downward) << 16))
    return ((misses & 0xFFFF) == 0) | ((misses >> 16) == 0)


def local(
    sectors, bonds,
    psi, left_env, right_env, sector_label, charge_step, coef_index, entry_values, recurrence,
):
    operands = (
        sector_label, charge_step.transpose(2, 0, 1), coef_index.transpose(2, 0, 1), entry_values, recurrence,
        left_env[0, 0], right_env[0, 0], psi[0],
    )
    vec_one, vec_two = lax.cond(
        one_block_per_plane(sector_label),
        lambda: lean_call(sectors, bonds, operands),
        lambda: both(False, sectors, bonds, operands),
    )
    return (vec_one[None], vec_two[None])


def solution(mesh):
    in_specs = (
        P("sector", None, None),
        P("mpo", "sector", None, None),
        P("mpo", "sector", None, None),
        P(),
        P(),
        P(),
        P(),
        P(),
    )
    out_specs = (P("sector", None, None), P("sector", None, None))
    body = functools.partial(local, mesh.shape["sector"], mesh.shape["mpo"])
    return jax.shard_map(body, mesh=mesh, in_specs=in_specs, out_specs=out_specs, check_vma=False)
```
